32 devices in a mesh: dp: 8 (over z, y), ctx: 2 (over x), tensor: 2 (over core).
Axes of the slice: x: 2, y: 2, z: 4, core: 2. Of those that a mesh axis runs over, the one named last changes fastest.
Arguments:
- block_input: bfloat16 [8, 384, 1024], P('dp', 'ctx'), may hold values from -6 to 6
- attn_gain: float32 [1024], replicated, may hold values from 0.1 to 1.9
- query_weight: bfloat16 [1024, 2048], P('dp', 'tensor'), may hold values from -0.1875 to 0.1875
- key_weight: bfloat16 [1024, 1024], P('dp', 'tensor'), may hold values from -0.1875 to 0.1875
- value_weight: bfloat16 [1024, 1024], P('dp', 'tensor'), may hold values from -0.1875 to 0.1875
- query_gain: float32 [128], replicated, may hold values from 0.5 to 12
- key_gain: float32 [128], replicated, may hold values from 0.5 to 12
- output_weight: bfloat16 [2048, 1024], P('tensor', 'dp'), may hold values from -1 to 1
- mlp_gain: float32 [1024], replicated, may hold values from 0.1 to 1.9
- gate_weight: bfloat16 [1024, 3072], P('dp', 'tensor'), may hold values from -0.1875 to 0.1875
- up_weight: bfloat16 [1024, 3072], P('dp', 'tensor'), may hold values from -0.1875 to 0.1875
- down_weight: bfloat16 [3072, 1024], P('tensor', 'dp'), may hold values from -0.109375 to 0.109375
- cotangent: bfloat16 [8, 384, 1024], P('dp', 'ctx'), may hold values from -6 to 6
Outputs:
- block_output: bfloat16 [8, 384, 1024], P('dp', 'ctx')
- input_grad: bfloat16 [8, 384, 1024], P('dp', 'ctx')
- attn_gain_grad: float32 [1024], P('dp')
- query_weight_grad: float32 [1024, 2048], P('dp', 'tensor')
- key_weight_grad: float32 [1024, 1024], P('dp', 'tensor')
- value_weight_grad: float32 [1024, 1024], P('dp', 'tensor')
- query_gain_grad: float32 [128], P('dp')
- key_gain_grad: float32 [128], P('dp')
- output_weight_grad: float32 [2048, 1024], P('tensor', 'dp')
- mlp_gain_grad: float32 [1024], P('dp')
- gate_weight_grad: float32 [1024, 3072], P('dp', 'tensor')
- up_weight_grad: float32 [1024, 3072], P('dp', 'tensor')
- down_weight_grad: float32 [3072, 1024], P('tensor', 'dp')
The draws below stay inside these ranges and needn't reach their ends.
All inputs are finite; a program needn't handle non-finite values.
Results may differ from the reference program's by a relative error of at most 0.015.
The reference program's roundings to bfloat16 on the way count: a program that leaves them out, or rounds other values in their place, can miss the bound.
Values may be sent and summed in bfloat16 or wider, within the bound.
A program may use at most 128 MiB of HBM per device.

```python
import math
import jax
import jax.numpy as jnp
from jax import lax

D = 1024
HEADS = 16
KVH = 8
HD = 128
FF = 3072
BLK = 192
LEN = 384
SEQS = 8
N_CTX = 2


def spread_gain(key, salt):
    level = jax.random.uniform(jax.random.fold_in(key, salt), (HD,), jnp.float32, -0.6931, 0.6931)
    return jnp.exp(level)


def draw_query_gain(key, part):
    values = spread_gain(key, 1)
    return values


def draw_key_gain(key, part):
    values = spread_gain(key, 3)
    return values


def steps_of(key, dims, cuts, low, largest):
    level, own = 1.0, jax.random.fold_in(key, 6)
    for axis_at, parts in cuts:
        steps = jnp.exp(jax.random.uniform(jax.random.fold_in(own, axis_at), (parts,), jnp.float32, low / len(cuts), largest / len(cuts)))
        level = level * jnp.repeat(steps, dims[axis_at] // parts).reshape([-1 if axis == axis_at else 1 for axis in range(len(dims))])
    return level


def scatter_about(key, dims, spread, reach, cuts=(), kind=jnp.bfloat16):
    values = jax.random.normal(key, dims, jnp.float32) * spread
    if len(cuts) > 0:
        values = steps_of(key, dims, cuts, -0.22, 0.18) * values
    return jnp.clip(values, min=-reach, max=reach).astype(kind)


def setup_inputs(seed: int = 0) -> dict:
    key_list = jax.random.split(jax.random.key(seed), 14)
    return {
        "block_input": scatter_about(key_list[0], (SEQS, LEN, D), 1.0, 6.0, ((0, 8), (1, 2))),
        "attn_gain": jnp.clip(1.0 + 0.18 * jax.random.normal(key_list[1], (D,), jnp.float32), 0.1, 1.9),
        "query_weight": scatter_about(key_list[2], (D, HEADS * HD), D ** -0.5, 0.1875, ((0, 8), (1, 2))),
        "key_weight": scatter_about(key_list[3], (D, KVH * HD), D ** -0.5, 0.1875, ((0, 8), (1, 2))),
        "value_weight": scatter_about(key_list[4], (D, KVH * HD), D ** -0.5, 0.1875, ((0, 8), (1, 2))),
        "query_gain": draw_query_gain(jax.random.fold_in(key_list[13], 71), 0),
        "key_gain": draw_key_gain(jax.random.fold_in(key_list[13], 71), 0),
        "output_weight": scatter_about(key_list[7], (HEADS * HD, D), (max(1, 6 * HEADS * HD // (BLK * N_CTX))) ** -0.5, 1.0, ((0, 2), (1, 8))),
        "mlp_gain": jnp.clip(1.0 + 0.18 * jax.random.normal(key_list[8], (D,), jnp.float32), 0.1, 1.9),
        "gate_weight": scatter_about(key_list[9], (D, FF), D ** -0.5, 0.1875, ((0, 8), (1, 2))),
        "up_weight": scatter_about(key_list[10], (D, FF), D ** -0.5, 0.1875, ((0, 8), (1, 2))),
        "down_weight": scatter_about(key_list[11], (FF, D), FF ** -0.5, 0.109375, ((0, 2), (1, 8))),
        "cotangent": scatter_about(key_list[12], (SEQS, LEN, D), 1.0, 6.0, ((0, 8), (1, 2))),
    }


EPS = 1e-06
THETA = 1000000.0
F32 = jnp.float32
BF16 = jnp.bfloat16

def rounded(value):
    return lax.optimization_barrier(value.astype(BF16)).astype(F32)

def rms_inverse(value):
    return lax.rsqrt(lax.optimization_barrier(jnp.mean(value * value, axis=-1, keepdims=True)) + EPS)

def norm_back(grad, unit, inverse, gain):
    scaled = grad * gain
    return inverse * (scaled - unit * lax.optimization_barrier(jnp.mean(scaled * unit, axis=-1, keepdims=True)))

def rotate(value):
    half_width = value.shape[-1] // 2
    return jnp.concatenate([-value[..., half_width:], value[..., :half_width]], axis=-1)

def rotate_back(value):
    half_width = value.shape[-1] // 2
    return jnp.concatenate([value[..., half_width:], -value[..., :half_width]], axis=-1)

def rope_tables(positions, width):
    half_width = width // 2
    exponent = jnp.arange(half_width).astype(F32) * (2.0 / width)
    frequency = jnp.power(THETA, -exponent)
    angle = positions.astype(F32)[:, None] * frequency[None, :]
    angle = jnp.concatenate([angle, angle], axis=-1)
    return (jnp.cos(angle), jnp.sin(angle))

def one_sequence(x_seq, dy_seq, params):
    attn_gain, w_query, w_key, w_value, query_gain, key_gain, w_out, mlp_gain, w_gate, w_up, w_down = params
    length = x_seq.shape[0]
    group_size = HEADS // KVH
    score_scale = 1.0 / math.sqrt(HD)
    positions = jnp.arange(length).astype(jnp.int32)
    cos_table, sin_table = rope_tables(positions, HD)
    cos_heads = cos_table[:, None, :]
    sin_heads = sin_table[:, None, :]
    tokens = x_seq.astype(F32)
    inv_one = rms_inverse(tokens)
    unit_one = tokens * inv_one
    normed_one = (unit_one * attn_gain).astype(BF16)
    query = jnp.dot(normed_one, w_query, preferred_element_type=F32).reshape(length, HEADS, HD)
    key_raw = jnp.dot(normed_one, w_key, preferred_element_type=F32).reshape(length, KVH, HD)
    value = jnp.dot(normed_one, w_value, preferred_element_type=F32).astype(BF16).reshape(length, KVH, HD)
    query_inv = rms_inverse(query)
    query_unit = query * query_inv
    query_scaled = query_unit * query_gain
    query_rot = (query_scaled * cos_heads + rotate(query_scaled) * sin_heads).astype(BF16)
    key_inv = rms_inverse(key_raw)
    key_unit = key_raw * key_inv
    key_scaled = key_unit * key_gain
    key_rot = (key_scaled * cos_heads + rotate(key_scaled) * sin_heads).astype(BF16)
    q_heads = query_rot.reshape(length, KVH, group_size, HD).transpose(1, 2, 0, 3)
    k_heads = key_rot.transpose(1, 0, 2)
    v_heads = value.transpose(1, 0, 2)
    allowed = positions[:, None] >= positions[None, :]

    def head_scores(q_one, k_one):
        raw_scores = jnp.einsum('gqd,nd->gqn', q_one.astype(F32), k_one.astype(F32)) * score_scale
        return jnp.where(allowed[None], raw_scores, -jnp.inf)

    def head_forward(item):
        q_one, k_one, v_one = item
        scores = head_scores(q_one, k_one)
        row_peak = lax.optimization_barrier(jnp.max(scores, axis=-1))
        expo = jnp.exp(scores - row_peak[..., None])
        row_total = lax.optimization_barrier(jnp.sum(expo, axis=-1))
        mixed = jnp.einsum('gqn,nd->gqd', rounded(expo), v_one.astype(F32)) / row_total[..., None]
        return (mixed.astype(BF16), row_peak + jnp.log(row_total))
    attn_heads, log_total = lax.map(head_forward, (q_heads, k_heads, v_heads))
    attn = attn_heads.transpose(2, 0, 1, 3).reshape(length, HEADS * HD)
    resid = tokens + jnp.dot(attn, w_out, preferred_element_type=F32)
    inv_two = rms_inverse(resid)
    unit_two = resid * inv_two
    normed_two = (unit_two * mlp_gain).astype(BF16)
    gate = jnp.dot(normed_two, w_gate, preferred_element_type=F32)
    up_proj = jnp.dot(normed_two, w_up, preferred_element_type=F32)
    sigma = jax.nn.sigmoid(gate)
    silu_gate = gate * sigma
    hidden = (silu_gate * up_proj).astype(BF16)
    output = (resid + jnp.dot(hidden, w_down, preferred_element_type=F32)).astype(BF16)
    d_hidden = jnp.dot(dy_seq, w_down.T, preferred_element_type=F32)
    grad_down = jnp.dot(hidden.T, dy_seq, preferred_element_type=F32)
    d_gate = (d_hidden * up_proj * sigma * (1.0 + gate * (1.0 - sigma))).astype(BF16)
    d_up = (d_hidden * silu_gate).astype(BF16)
    grad_gate = jnp.dot(normed_two.T, d_gate, preferred_element_type=F32)
    grad_up = jnp.dot(normed_two.T, d_up, preferred_element_type=F32)
    d_normed_two = jnp.dot(d_gate, w_gate.T, preferred_element_type=F32) + jnp.dot(d_up, w_up.T, preferred_element_type=F32)
    grad_mlp_gain = lax.optimization_barrier(jnp.sum(d_normed_two * unit_two, axis=0))
    d_resid = dy_seq.astype(F32) + norm_back(d_normed_two, unit_two, inv_two, mlp_gain)
    d_resid_b = d_resid.astype(BF16)
    grad_out = jnp.dot(attn.T, d_resid_b, preferred_element_type=F32)
    d_attn = jnp.dot(d_resid_b, w_out.T, preferred_element_type=F32).astype(BF16)
    delta = lax.optimization_barrier(jnp.sum(d_attn.astype(F32).reshape(length, HEADS, HD) * attn.astype(F32).reshape(length, HEADS, HD), axis=-1))
    da_heads = d_attn.reshape(length, KVH, group_size, HD).transpose(1, 2, 0, 3)
    delta_heads = delta.reshape(length, KVH, group_size).transpose(1, 2, 0)

    def head_backward(item):
        q_one, k_one, v_one, da_one, lse_one, delta_one = item
        scores = head_scores(q_one, k_one)
        probs = jnp.exp(scores - lse_one[..., None])
        d_probs = jnp.einsum('gqd,nd->gqn', da_one.astype(F32), v_one.astype(F32))
        d_scores = rounded(probs * (d_probs - delta_one[..., None]) * score_scale)
        d_q = jnp.einsum('gqn,nd->gqd', d_scores, k_one.astype(F32))
        d_k = jnp.einsum('gqn,gqd->nd', d_scores, q_one.astype(F32))
        d_v = jnp.einsum('gqn,gqd->nd', rounded(probs), da_one.astype(F32))
        return (d_q, d_k, d_v)
    dq_heads, dk_heads, dv_heads = lax.map(head_backward, (q_heads, k_heads, v_heads, da_heads, log_total, delta_heads))
    d_query_rot = dq_heads.transpose(2, 0, 1, 3).reshape(length, HEADS, HD)
    d_key_rot = dk_heads.transpose(1, 0, 2)
    d_value = dv_heads.transpose(1, 0, 2).reshape(length, KVH * HD).astype(BF16)
    d_query_scaled = d_query_rot * cos_heads + rotate_back(d_query_rot * sin_heads)
    d_key_scaled = d_key_rot * cos_heads + rotate_back(d_key_rot * sin_heads)
    grad_query_gain = lax.optimization_barrier(jnp.sum(d_query_scaled * query_unit, axis=(0, 1)))
    grad_key_gain = lax.optimization_barrier(jnp.sum(d_key_scaled * key_unit, axis=(0, 1)))
    d_query = norm_back(d_query_scaled, query_unit, query_inv, query_gain).astype(BF16).reshape(length, HEADS * HD)
    d_key = norm_back(d_key_scaled, key_unit, key_inv, key_gain).astype(BF16).reshape(length, KVH * HD)
    grad_query = jnp.dot(normed_one.T, d_query, preferred_element_type=F32)
    grad_key = jnp.dot(normed_one.T, d_key, preferred_element_type=F32)
    grad_value = jnp.dot(normed_one.T, d_value, preferred_element_type=F32)
    d_normed_one = jnp.dot(d_query, w_query.T, preferred_element_type=F32)
    d_normed_one = d_normed_one + jnp.dot(d_key, w_key.T, preferred_element_type=F32)
    d_normed_one = d_normed_one + jnp.dot(d_value, w_value.T, preferred_element_type=F32)
    grad_attn_gain = lax.optimization_barrier(jnp.sum(d_normed_one * unit_one, axis=0))
    d_input = (d_resid + norm_back(d_normed_one, unit_one, inv_one, attn_gain)).astype(BF16)
    grads = (grad_attn_gain, grad_query, grad_key, grad_value, grad_query_gain, grad_key_gain, grad_out, grad_mlp_gain, grad_gate, grad_up, grad_down)
    return (output, d_input, grads)

def zeros_like_float(weight):
    return jnp.zeros(weight.shape, F32)

def reference(block_input, attn_gain, query_weight, key_weight, value_weight, query_gain, key_gain, output_weight, mlp_gain, gate_weight, up_weight, down_weight, cotangent):
    params = (attn_gain, query_weight, key_weight, value_weight, query_gain, key_gain, output_weight, mlp_gain, gate_weight, up_weight, down_weight)
    start_grads = jax.tree.map(zeros_like_float, params)

    def step_sequence(carry, item):
        x_seq, dy_seq = item
        output, d_input, grads = one_sequence(x_seq, dy_seq, params)
        return (jax.tree.map(jnp.add, carry, grads), (output, d_input))
    totals, stacked = lax.scan(step_sequence, start_grads, (block_input, cotangent))
    outputs, d_inputs = stacked
    return (outputs, d_inputs, totals[0], totals[1], totals[2], totals[3], totals[4], totals[5], totals[6], totals[7], totals[8], totals[9], totals[10])
```

```python
import functools
import math

import jax
import jax.numpy as jnp
from jax import lax
from jax.sharding import PartitionSpec as P

HD = 128


EPS = 1e-06
THETA = 1000000.0
F32 = jnp.float32
BF16 = jnp.bfloat16


def rms_inverse(value):
    return lax.rsqrt(jnp.mean(value * value, axis=-1, keepdims=True) + EPS)


def norm_back(grad, unit, inverse, gain):
    scaled = grad * gain
    return inverse * (scaled - unit * jnp.mean(scaled * unit, axis=-1, keepdims=True))


def rotate(value):
    half_width = value.shape[-1] // 2
    return jnp.concatenate([-value[..., half_width:], value[..., :half_width]], axis=-1)


def rotate_back(value):
    half_width = value.shape[-1] // 2
    return jnp.concatenate([value[..., half_width:], -value[..., :half_width]], axis=-1)


def rope_tables(positions, width):
    half_width = width // 2
    exponent = jnp.arange(half_width).astype(F32) * (2.0 / width)
    frequency = jnp.power(THETA, -exponent)
    angle = positions.astype(F32)[:, None] * frequency[None, :]
    angle = jnp.concatenate([angle, angle], axis=-1)
    return (jnp.cos(angle), jnp.sin(angle))


def over_heads(partial_value):
    return lax.psum(partial_value, "tensor")


def per_device(
    block_input,
    attn_gain,
    query_weight,
    key_weight,
    value_weight,
    query_gain,
    key_gain,
    output_weight,
    mlp_gain,
    gate_weight,
    up_weight,
    down_weight,
    cotangent,
):
    tokens = block_input[0].astype(F32)
    row_count = tokens.shape[0]
    score_scale = 1.0 / math.sqrt(HD)
    positions = lax.axis_index("ctx") * row_count + jnp.arange(row_count, dtype=jnp.int32)
    cos_table, sin_table = rope_tables(positions, HD)
    cos_heads = cos_table[:, None, :]
    sin_heads = sin_table[:, None, :]
    w_query, w_key, w_value, w_out, w_gate, w_up, w_down = (
        lax.all_gather(query_weight, "dp", axis=0, tiled=True),
        lax.all_gather(key_weight, "dp", axis=0, tiled=True),
        lax.all_gather(value_weight, "dp", axis=0, tiled=True),
        lax.all_gather(output_weight, "dp", axis=1, tiled=True),
        lax.all_gather(gate_weight, "dp", axis=0, tiled=True),
        lax.all_gather(up_weight, "dp", axis=0, tiled=True),
        lax.all_gather(down_weight, "dp", axis=1, tiled=True),
    )
    q_heads = w_query.shape[1] // HD
    kv_heads = w_key.shape[1] // HD
    group_size = q_heads // kv_heads
    inv_one = rms_inverse(tokens)
    unit_one = tokens * inv_one
    normed_one = (unit_one * attn_gain).astype(BF16)
    query = jnp.dot(normed_one, w_query, preferred_element_type=F32).reshape(row_count, q_heads, HD)
    key_raw = jnp.dot(normed_one, w_key, preferred_element_type=F32).reshape(
        row_count, kv_heads, HD
    )
    value = (
        jnp.dot(normed_one, w_value, preferred_element_type=F32)
        .astype(BF16)
        .reshape(row_count, kv_heads, HD)
    )
    query_inv = rms_inverse(query)
    query_unit = query * query_inv
    query_scaled = query_unit * query_gain
    query_rot = (query_scaled * cos_heads + rotate(query_scaled) * sin_heads).astype(BF16)
    key_inv = rms_inverse(key_raw)
    key_unit = key_raw * key_inv
    key_scaled = key_unit * key_gain
    key_rot = (key_scaled * cos_heads + rotate(key_scaled) * sin_heads).astype(BF16)
    grouped_query = query_rot.reshape(row_count, kv_heads, group_size, HD)

    def piece_scores(piece_keys):
        piece_rows = piece_keys.shape[0]
        key_positions = jnp.arange(piece_rows, dtype=jnp.int32)
        allowed = key_positions[None, :] <= positions[:, None]
        scores = (
            jnp.einsum("qkgd,nkd->kgqn", grouped_query, piece_keys, preferred_element_type=F32)
            * score_scale
        )
        return jnp.where(allowed, scores, -jnp.inf)

    peak_old = jnp.full((kv_heads, group_size, row_count), -1e30, F32)
    piece_keys = lax.all_gather(key_rot, "ctx", axis=0, tiled=True)
    piece_values = lax.all_gather(value, "ctx", axis=0, tiled=True)
    scores = piece_scores(piece_keys)
    peak_new = jnp.maximum(peak_old, jnp.max(scores, axis=-1))
    expo = jnp.exp(scores - peak_new[..., None])
    total_new = jnp.sum(expo, axis=-1)
    accum_new = jnp.einsum(
        "kgqn,nkd->kgqd", expo.astype(BF16), piece_values, preferred_element_type=F32
    )
    log_total = peak_new + jnp.log(total_new)
    attn = (
        (accum_new / total_new[..., None])
        .astype(BF16)
        .transpose(2, 0, 1, 3)
        .reshape(row_count, q_heads * HD)
    )
    resid = tokens + over_heads(jnp.dot(attn, w_out, preferred_element_type=F32))
    inv_two = rms_inverse(resid)
    unit_two = resid * inv_two
    normed_two = (unit_two * mlp_gain).astype(BF16)
    gate = jnp.dot(normed_two, w_gate, preferred_element_type=F32)
    up_proj = jnp.dot(normed_two, w_up, preferred_element_type=F32)
    sigma = jax.nn.sigmoid(gate)
    silu_gate = gate * sigma
    hidden = (silu_gate * up_proj).astype(BF16)
    output = (resid + over_heads(jnp.dot(hidden, w_down, preferred_element_type=F32))).astype(BF16)
    w_query, w_key, w_value, w_out, w_gate, w_up, w_down = (
        lax.all_gather(query_weight, "dp", axis=0, tiled=True),
        lax.all_gather(key_weight, "dp", axis=0, tiled=True),
        lax.all_gather(value_weight, "dp", axis=0, tiled=True),
        lax.all_gather(output_weight, "dp", axis=1, tiled=True),
        lax.all_gather(gate_weight, "dp", axis=0, tiled=True),
        lax.all_gather(up_weight, "dp", axis=0, tiled=True),
        lax.all_gather(down_weight, "dp", axis=1, tiled=True),
    )
    d_output = cotangent[0]
    d_hidden = jnp.einsum("td,fd->tf", d_output, w_down, preferred_element_type=F32)
    grad_down = jnp.einsum("tf,td->fd", hidden, d_output, preferred_element_type=F32)
    d_gate = (d_hidden * up_proj * sigma * (1.0 + gate * (1.0 - sigma))).astype(BF16)
    d_up = (d_hidden * silu_gate).astype(BF16)
    grad_gate = jnp.einsum("td,tf->df", normed_two, d_gate, preferred_element_type=F32)
    grad_up = jnp.einsum("td,tf->df", normed_two, d_up, preferred_element_type=F32)
    partial_two = jnp.einsum("tf,df->td", d_gate, w_gate, preferred_element_type=F32) + jnp.einsum(
        "tf,df->td", d_up, w_up, preferred_element_type=F32
    )
    d_normed_two = lax.psum(partial_two, "tensor")
    grad_mlp_gain = jnp.sum(d_normed_two * unit_two, axis=0)
    d_resid = d_output.astype(F32) + norm_back(d_normed_two, unit_two, inv_two, mlp_gain)
    d_resid_b = d_resid.astype(BF16)
    grad_out = jnp.einsum("th,td->hd", attn, d_resid_b, preferred_element_type=F32)
    d_attn = jnp.einsum("td,hd->th", d_resid_b, w_out, preferred_element_type=F32).astype(BF16)
    delta = jnp.sum(
        d_attn.astype(F32).reshape(row_count, q_heads, HD)
        * attn.astype(F32).reshape(row_count, q_heads, HD),
        axis=-1,
    )
    delta_heads = delta.reshape(row_count, kv_heads, group_size).transpose(1, 2, 0)
    grouped_grad = d_attn.reshape(row_count, kv_heads, group_size, HD)
    piece_keys = lax.all_gather(key_rot, "ctx", axis=0, tiled=True)
    piece_values = lax.all_gather(value, "ctx", axis=0, tiled=True)
    piece_rows = piece_keys.shape[0]
    scores = piece_scores(piece_keys)
    probs = jnp.exp(scores - log_total[..., None])
    d_probs = jnp.einsum("qkgd,nkd->kgqn", grouped_grad, piece_values, preferred_element_type=F32)
    d_scores = (probs * (d_probs - delta_heads[..., None]) * score_scale).astype(BF16)
    d_query_acc = jnp.einsum("kgqn,nkd->kgqd", d_scores, piece_keys, preferred_element_type=F32)
    d_key_piece = jnp.einsum("kgqn,qkgd->nkd", d_scores, grouped_query, preferred_element_type=F32)
    d_value_piece = jnp.einsum(
        "kgqn,qkgd->nkd", probs.astype(BF16), grouped_grad, preferred_element_type=F32
    )
    update = jnp.stack([d_key_piece, d_value_piece])
    d_kv_home = lax.psum_scatter(update, "ctx", scatter_dimension=1, tiled=True)
    d_query_rot = d_query_acc.transpose(2, 0, 1, 3).reshape(row_count, q_heads, HD)
    d_key_rot = d_kv_home[0]
    d_value = d_kv_home[1].astype(BF16).reshape(row_count, kv_heads * HD)
    d_query_scaled = d_query_rot * cos_heads + rotate_back(d_query_rot * sin_heads)
    d_key_scaled = d_key_rot * cos_heads + rotate_back(d_key_rot * sin_heads)
    query_gain_part = jnp.sum(d_query_scaled * query_unit, axis=(0, 1))
    key_gain_part = jnp.sum(d_key_scaled * key_unit, axis=(0, 1))
    d_query = (
        norm_back(d_query_scaled, query_unit, query_inv, query_gain)
        .astype(BF16)
        .reshape(row_count, q_heads * HD)
    )
    d_key = (
        norm_back(d_key_scaled, key_unit, key_inv, key_gain)
        .astype(BF16)
        .reshape(row_count, kv_heads * HD)
    )
    grad_query = jnp.einsum("td,th->dh", normed_one, d_query, preferred_element_type=F32)
    grad_key = jnp.einsum("td,th->dh", normed_one, d_key, preferred_element_type=F32)
    grad_value = jnp.einsum("td,th->dh", normed_one, d_value, preferred_element_type=F32)
    partial_one = jnp.einsum("th,dh->td", d_query, w_query, preferred_element_type=F32)
    partial_one = partial_one + jnp.einsum("th,dh->td", d_key, w_key, preferred_element_type=F32)
    partial_one = partial_one + jnp.einsum(
        "th,dh->td", d_value, w_value, preferred_element_type=F32
    )
    d_normed_one, query_gain_heads, key_gain_heads = lax.psum(
        (partial_one, query_gain_part, key_gain_part), "tensor"
    )
    grad_attn_gain = jnp.sum(d_normed_one * unit_one, axis=0)
    d_input = (d_resid + norm_back(d_normed_one, unit_one, inv_one, attn_gain)).astype(BF16)
    (
        share_a,
        share_q,
        share_k,
        share_v,
        share_qg,
        share_kg,
        share_o,
        share_m,
        share_g,
        share_u,
        share_d,
    ) = (
        lax.psum_scatter(grad_attn_gain, "dp", scatter_dimension=0, tiled=True),
        lax.psum_scatter(grad_query, "dp", scatter_dimension=0, tiled=True),
        lax.psum_scatter(grad_key, "dp", scatter_dimension=0, tiled=True),
        lax.psum_scatter(grad_value, "dp", scatter_dimension=0, tiled=True),
        lax.psum_scatter(query_gain_heads, "dp", scatter_dimension=0, tiled=True),
        lax.psum_scatter(key_gain_heads, "dp", scatter_dimension=0, tiled=True),
        lax.psum_scatter(grad_out, "dp", scatter_dimension=1, tiled=True),
        lax.psum_scatter(grad_mlp_gain, "dp", scatter_dimension=0, tiled=True),
        lax.psum_scatter(grad_gate, "dp", scatter_dimension=0, tiled=True),
        lax.psum_scatter(grad_up, "dp", scatter_dimension=0, tiled=True),
        lax.psum_scatter(grad_down, "dp", scatter_dimension=1, tiled=True),
    )
    finals = lax.psum(
        (
            share_a,
            share_q,
            share_k,
            share_v,
            share_qg,
            share_kg,
            share_o,
            share_m,
            share_g,
            share_u,
            share_d,
        ),
        "ctx",
    )
    return (
        output[None],
        d_input[None],
        finals[0],
        finals[1],
        finals[2],
        finals[3],
        finals[4],
        finals[5],
        finals[6],
        finals[7],
        finals[8],
        finals[9],
        finals[10],
    )


def tree_exchange(value, axis_name, axis_size):
    return lax.ppermute(value, axis_name, [(i, i ^ 1) for i in range(axis_size)])


def paired_device(
    dp_size,
    block_input,
    attn_gain,
    query_weight,
    key_weight,
    value_weight,
    query_gain,
    key_gain,
    output_weight,
    mlp_gain,
    gate_weight,
    up_weight,
    down_weight,
    cotangent,
):
    line = dp_size // 2
    line_groups = [[2 * j + side for j in range(line)] for side in range(2)]
    side = lax.axis_index("dp") % 2
    block = lax.axis_index("ctx")
    owned = query_weight.shape[0]
    width = owned * dp_size

    def to_ctx(value):
        return tree_exchange(value, "ctx", 2)

    def to_pair(value):
        return tree_exchange(value, "dp", dp_size)

    def over_tensor(value):
        return value + tree_exchange(value, "tensor", 2)

    def to_local(value):
        split = value.reshape(value.shape[:-1] + (line, 2, owned))
        first, second = split[..., 0, :], split[..., 1, :]
        ordered = jnp.where(
            side == 0,
            jnp.stack([first, second], axis=-3),
            jnp.stack([second, first], axis=-3),
        )
        return ordered.reshape(value.shape)

    def from_local(value):
        split = value.reshape(value.shape[:-1] + (2, line, owned))
        first, second = split[..., 0, :, :], split[..., 1, :, :]
        ordered = jnp.where(
            side == 0,
            jnp.stack([first, second], axis=-2),
            jnp.stack([second, first], axis=-2),
        )
        return ordered.reshape(value.shape)

    def own_half(shard):
        half = shard.shape[1] // 2
        return lax.dynamic_slice_in_dim(shard, block * half, half, axis=1)

    def gather_line(shard):
        return lax.all_gather(
            shard, "dp", axis_index_groups=line_groups, axis=0, tiled=True
        )

    def spread_pair_first(part):
        part = jnp.concatenate([part, to_pair(part)], axis=0)
        return part, to_ctx(part)

    def spread_ctx_first(part):
        other = to_ctx(part)
        return (
            jnp.concatenate([part, to_pair(part)], axis=0),
            jnp.concatenate([other, to_pair(other)], axis=0),
        )

    halves = [own_half(shard) for shard in (query_weight, key_weight, value_weight)]
    cut_q = halves[0].shape[1]
    cut_k = cut_q + halves[1].shape[1]
    own_qkv, other_qkv = spread_pair_first(gather_line(jnp.concatenate(halves, axis=1)))

    def both(low, high):
        return jnp.concatenate([own_qkv[:, low:high], other_qkv[:, low:high]], axis=1)

    w_query, w_key, w_value = both(0, cut_q), both(cut_q, cut_k), both(cut_k, own_qkv.shape[1])
    w_out_t = jnp.concatenate(
        spread_ctx_first(gather_line(own_half(output_weight.T))), axis=1
    )
    w_gate = jnp.concatenate(spread_ctx_first(gather_line(own_half(gate_weight))), axis=1)
    w_up = jnp.concatenate(spread_pair_first(gather_line(own_half(up_weight))), axis=1)
    w_down_t = jnp.concatenate(spread_ctx_first(gather_line(own_half(down_weight.T))), axis=1)

    def both_blocks(value):
        half = value.shape[1] // 2
        return jnp.concatenate([value[:, :half], to_ctx(value[:, half:])], axis=0)

    def feature_side(value):
        value = jnp.concatenate([value, to_ctx(value)], axis=0)
        half = value.shape[1] // 2
        return jnp.concatenate([value[:, :half], to_pair(value[:, half:])], axis=0)

    def column_side(value):
        value = both_blocks(value)
        return jnp.concatenate([value, to_pair(value)], axis=0)

    def weight_share(features, columns):
        part = jnp.einsum("td,tf->df", features, columns, preferred_element_type=F32)
        share = lax.psum_scatter(
            part, "dp", axis_index_groups=line_groups, scatter_dimension=0, tiled=True
        )
        return share, to_ctx(share)

    def whole(share, other):
        return jnp.where(
            block == 0,
            jnp.concatenate([share, other], axis=1),
            jnp.concatenate([other, share], axis=1),
        )

    def mul_t(value, weight):
        return jnp.einsum("tf,df->td", value, weight, preferred_element_type=F32)

    row_count = block_input.shape[1]
    score_scale = 1.0 / math.sqrt(HD)
    attn_gain = to_local(attn_gain)
    mlp_gain = to_local(mlp_gain)
    tokens = to_local(block_input[0]).astype(F32)
    d_output = to_local(cotangent[0])
    positions = block * row_count + jnp.arange(row_count, dtype=jnp.int32)
    other_positions = (1 - block) * row_count + jnp.arange(row_count, dtype=jnp.int32)
    cos_table, sin_table = rope_tables(positions, HD)
    cos_heads = cos_table[:, None, :]
    sin_heads = sin_table[:, None, :]
    q_heads = w_query.shape[1] // HD
    kv_heads = w_key.shape[1] // HD
    group_size = q_heads // kv_heads

    inv_one = rms_inverse(tokens)
    unit_one = tokens * inv_one
    normed_one = (unit_one * attn_gain).astype(BF16)
    query = jnp.dot(normed_one, w_query, preferred_element_type=F32).reshape(row_count, q_heads, HD)
    key_raw = jnp.dot(normed_one, w_key, preferred_element_type=F32).reshape(
        row_count, kv_heads, HD
    )
    value = (
        jnp.dot(normed_one, w_value, preferred_element_type=F32)
        .astype(BF16)
        .reshape(row_count, kv_heads, HD)
    )
    query_inv = rms_inverse(query)
    query_unit = query * query_inv
    query_scaled = query_unit * query_gain
    query_rot = (query_scaled * cos_heads + rotate(query_scaled) * sin_heads).astype(BF16)
    key_inv = rms_inverse(key_raw)
    key_unit = key_raw * key_inv
    key_scaled = key_unit * key_gain
    key_rot = (key_scaled * cos_heads + rotate(key_scaled) * sin_heads).astype(BF16)
    grouped_query = query_rot.reshape(row_count, kv_heads, group_size, HD)

    def swap_heads(array):
        half = array.shape[-2] // 2
        return jnp.concatenate([array[..., half:, :], array[..., :half, :]], axis=-2)

    other_keys = swap_heads(to_ctx(key_rot))
    other_values = swap_heads(to_ctx(value))
    all_keys = jnp.concatenate([key_rot, other_keys], axis=0)
    all_values = jnp.concatenate([value, other_values], axis=0)
    key_positions = jnp.concatenate([positions, other_positions])
    allowed = key_positions[None, :] <= positions[:, None]
    scores = (
        jnp.einsum("qkgd,nkd->kgqn", grouped_query, all_keys, preferred_element_type=F32)
        * score_scale
    )
    scores = jnp.where(allowed, scores, -jnp.inf)
    peak = jnp.max(scores, axis=-1)
    expo = jnp.exp(scores - peak[..., None])
    total = jnp.sum(expo, axis=-1)
    accum = jnp.einsum("kgqn,nkd->kgqd", expo.astype(BF16), all_values, preferred_element_type=F32)
    log_total = peak + jnp.log(total)
    attn = (
        (accum / total[..., None])
        .astype(BF16)
        .transpose(2, 0, 1, 3)
        .reshape(row_count, q_heads * HD)
    )
    resid = tokens + over_tensor(mul_t(attn, w_out_t))
    inv_two = rms_inverse(resid)
    unit_two = resid * inv_two
    normed_two = (unit_two * mlp_gain).astype(BF16)
    gate = jnp.dot(normed_two, w_gate, preferred_element_type=F32)
    up_proj = jnp.dot(normed_two, w_up, preferred_element_type=F32)
    sigma = jax.nn.sigmoid(gate)
    silu_gate = gate * sigma
    hidden = (silu_gate * up_proj).astype(BF16)
    output = from_local((resid + over_tensor(mul_t(hidden, w_down_t))).astype(BF16))

    share_down = weight_share(feature_side(d_output), column_side(hidden))
    d_hidden = jnp.dot(d_output, w_down_t, preferred_element_type=F32)
    d_gate = (d_hidden * up_proj * sigma * (1.0 + gate * (1.0 - sigma))).astype(BF16)
    d_up = (d_hidden * silu_gate).astype(BF16)
    features_two = feature_side(normed_two)
    share_gate = weight_share(features_two, column_side(d_gate))
    share_up = weight_share(features_two, column_side(d_up))
    d_normed_two = over_tensor(mul_t(d_gate, w_gate) + mul_t(d_up, w_up))
    grad_mlp_gain = jnp.sum(d_normed_two * unit_two, axis=0)
    d_resid = d_output.astype(F32) + norm_back(d_normed_two, unit_two, inv_two, mlp_gain)
    d_resid_b = d_resid.astype(BF16)
    share_out = weight_share(feature_side(d_resid_b), column_side(attn))
    d_attn = jnp.dot(d_resid_b, w_out_t, preferred_element_type=F32).astype(BF16)
    delta = jnp.sum(
        d_attn.astype(F32).reshape(row_count, q_heads, HD)
        * attn.astype(F32).reshape(row_count, q_heads, HD),
        axis=-1,
    )
    delta_heads = delta.reshape(row_count, kv_heads, group_size).transpose(1, 2, 0)
    grouped_grad = d_attn.reshape(row_count, kv_heads, group_size, HD)
    probs = jnp.exp(scores - log_total[..., None])
    d_probs = jnp.einsum("qkgd,nkd->kgqn", grouped_grad, all_values, preferred_element_type=F32)
    d_scores = (probs * (d_probs - delta_heads[..., None]) * score_scale).astype(BF16)
    d_query_acc = jnp.einsum("kgqn,nkd->kgqd", d_scores, all_keys, preferred_element_type=F32)
    d_keys = jnp.einsum("kgqn,qkgd->nkd", d_scores, grouped_query, preferred_element_type=F32)
    d_values = jnp.einsum(
        "kgqn,qkgd->nkd", probs.astype(BF16), grouped_grad, preferred_element_type=F32
    )
    d_key_rot = d_keys[:row_count] + swap_heads(to_ctx(d_keys[row_count:]))
    d_value_sum = d_values[:row_count] + swap_heads(to_ctx(d_values[row_count:]))
    d_query_rot = d_query_acc.transpose(2, 0, 1, 3).reshape(row_count, q_heads, HD)
    d_value = d_value_sum.astype(BF16).reshape(row_count, kv_heads * HD)
    d_query_scaled = d_query_rot * cos_heads + rotate_back(d_query_rot * sin_heads)
    d_key_scaled = d_key_rot * cos_heads + rotate_back(d_key_rot * sin_heads)
    query_gain_part = jnp.sum(d_query_scaled * query_unit, axis=(0, 1))
    key_gain_part = jnp.sum(d_key_scaled * key_unit, axis=(0, 1))
    d_query = (
        norm_back(d_query_scaled, query_unit, query_inv, query_gain)
        .astype(BF16)
        .reshape(row_count, q_heads * HD)
    )
    d_key = (
        norm_back(d_key_scaled, key_unit, key_inv, key_gain)
        .astype(BF16)
        .reshape(row_count, kv_heads * HD)
    )
    features_one = feature_side(normed_one)
    columns_one = jnp.concatenate(
        [both_blocks(d_query), both_blocks(d_key), both_blocks(d_value)], axis=1
    )
    columns_one = jnp.concatenate([columns_one, to_pair(columns_one)], axis=0)
    share_qkv, other_qkv_share = weight_share(features_one, columns_one)
    d_normed_one = over_tensor(
        mul_t(d_query, w_query) + mul_t(d_key, w_key) + mul_t(d_value, w_value)
    )
    grad_attn_gain = jnp.sum(d_normed_one * unit_one, axis=0)
    d_input = from_local(
        (d_resid + norm_back(d_normed_one, unit_one, inv_one, attn_gain)).astype(BF16)
    )
    gains = lax.psum(
        jnp.concatenate(
            [
                from_local(0.5 * grad_attn_gain),
                from_local(0.5 * grad_mlp_gain),
                query_gain_part,
                key_gain_part,
            ]
        ),
        ("dp", "ctx", "tensor"),
    )
    owner = lax.axis_index("dp")

    def owned_gain(start, size):
        part = size // dp_size
        return lax.dynamic_slice_in_dim(gains, start + owner * part, part)

    def qkv_piece(low, high):
        return whole(share_qkv[:, low:high], other_qkv_share[:, low:high])

    return (
        output[None],
        d_input[None],
        owned_gain(0, width),
        qkv_piece(0, cut_q),
        qkv_piece(cut_q, cut_k),
        qkv_piece(cut_k, share_qkv.shape[1]),
        owned_gain(2 * width, HD),
        owned_gain(2 * width + HD, HD),
        whole(*share_out).T,
        owned_gain(width, width),
        whole(*share_gate),
        whole(*share_up),
        whole(*share_down).T,
    )


def solution(mesh):
    sizes = dict(mesh.shape)
    body = per_device
    if sizes["ctx"] == 2 and sizes["tensor"] == 2 and sizes["dp"] % 2 == 0:
        body = functools.partial(paired_device, sizes["dp"])
    return jax.shard_map(
        body,
        mesh=mesh,
        in_specs=(
            P("dp", "ctx", None),
            P(),
            P("dp", "tensor"),
            P("dp", "tensor"),
            P("dp", "tensor"),
            P(),
            P(),
            P("tensor", "dp"),
            P(),
            P("dp", "tensor"),
            P("dp", "tensor"),
            P("tensor", "dp"),
            P("dp", "ctx", None),
        ),
        out_specs=(
            P("dp", "ctx", None),
            P("dp", "ctx", None),
            P("dp"),
            P("dp", "tensor"),
            P("dp", "tensor"),
            P("dp", "tensor"),
            P("dp"),
            P("dp"),
            P("tensor", "dp"),
            P("dp"),
            P("dp", "tensor"),
            P("dp", "tensor"),
            P("tensor", "dp"),
        ),
        check_vma=False,
    )
```

```python
import functools
import math

import jax
import jax.numpy as jnp
from jax import lax
from jax.sharding import PartitionSpec as P

HD = 128


EPS = 1e-06
THETA = 1000000.0
F32 = jnp.float32
BF16 = jnp.bfloat16


def rms_inverse(value):
    return lax.rsqrt(jnp.mean(value * value, axis=-1, keepdims=True) + EPS)


def norm_back(grad, unit, inverse, gain):
    scaled = grad * gain
    return inverse * (scaled - unit * jnp.mean(scaled * unit, axis=-1, keepdims=True))


def rotate(value):
    half_width = value.shape[-1] // 2
    return jnp.concatenate([-value[..., half_width:], value[..., :half_width]], axis=-1)


def rotate_back(value):
    half_width = value.shape[-1] // 2
    return jnp.concatenate([value[..., half_width:], -value[..., :half_width]], axis=-1)


def rope_tables(positions, width):
    half_width = width // 2
    exponent = jnp.arange(half_width).astype(F32) * (2.0 / width)
    frequency = jnp.power(THETA, -exponent)
    angle = positions.astype(F32)[:, None] * frequency[None, :]
    angle = jnp.concatenate([angle, angle], axis=-1)
    return (jnp.cos(angle), jnp.sin(angle))


def over_heads(partial_value):
    return lax.psum(partial_value, "tensor")


def per_device(
    block_input,
    attn_gain,
    query_weight,
    key_weight,
    value_weight,
    query_gain,
    key_gain,
    output_weight,
    mlp_gain,
    gate_weight,
    up_weight,
    down_weight,
    cotangent,
):
    tokens = block_input[0].astype(F32)
    row_count = tokens.shape[0]
    score_scale = 1.0 / math.sqrt(HD)
    positions = lax.axis_index("ctx") * row_count + jnp.arange(row_count, dtype=jnp.int32)
    cos_table, sin_table = rope_tables(positions, HD)
    cos_heads = cos_table[:, None, :]
    sin_heads = sin_table[:, None, :]
    w_query, w_key, w_value, w_out, w_gate, w_up, w_down = (
        lax.all_gather(query_weight, "dp", axis=0, tiled=True),
        lax.all_gather(key_weight, "dp", axis=0, tiled=True),
        lax.all_gather(value_weight, "dp", axis=0, tiled=True),
        lax.all_gather(output_weight, "dp", axis=1, tiled=True),
        lax.all_gather(gate_weight, "dp", axis=0, tiled=True),
        lax.all_gather(up_weight, "dp", axis=0, tiled=True),
        lax.all_gather(down_weight, "dp", axis=1, tiled=True),
    )
    q_heads = w_query.shape[1] // HD
    kv_heads = w_key.shape[1] // HD
    group_size = q_heads // kv_heads
    inv_one = rms_inverse(tokens)
    unit_one = tokens * inv_one
    normed_one = (unit_one * attn_gain).astype(BF16)
    query = jnp.dot(normed_one, w_query, preferred_element_type=F32).reshape(row_count, q_heads, HD)
    key_raw = jnp.dot(normed_one, w_key, preferred_element_type=F32).reshape(
        row_count, kv_heads, HD
    )
    value = (
        jnp.dot(normed_one, w_value, preferred_element_type=F32)
        .astype(BF16)
        .reshape(row_count, kv_heads, HD)
    )
    query_inv = rms_inverse(query)
    query_unit = query * query_inv
    query_scaled = query_unit * query_gain
    query_rot = (query_scaled * cos_heads + rotate(query_scaled) * sin_heads).astype(BF16)
    key_inv = rms_inverse(key_raw)
    key_unit = key_raw * key_inv
    key_scaled = key_unit * key_gain
    key_rot = (key_scaled * cos_heads + rotate(key_scaled) * sin_heads).astype(BF16)
    grouped_query = query_rot.reshape(row_count, kv_heads, group_size, HD)

    def piece_scores(piece_keys):
        piece_rows = piece_keys.shape[0]
        key_positions = jnp.arange(piece_rows, dtype=jnp.int32)
        allowed = key_positions[None, :] <= positions[:, None]
        scores = (
            jnp.einsum("qkgd,nkd->kgqn", grouped_query, piece_keys, preferred_element_type=F32)
            * score_scale
        )
        return jnp.where(allowed, scores, -jnp.inf)

    peak_old = jnp.full((kv_heads, group_size, row_count), -1e30, F32)
    piece_keys = lax.all_gather(key_rot, "ctx", axis=0, tiled=True)
    piece_values = lax.all_gather(value, "ctx", axis=0, tiled=True)
    scores = piece_scores(piece_keys)
    peak_new = jnp.maximum(peak_old, jnp.max(scores, axis=-1))
    expo = jnp.exp(scores - peak_new[..., None])
    total_new = jnp.sum(expo, axis=-1)
    accum_new = jnp.einsum(
        "kgqn,nkd->kgqd", expo.astype(BF16), piece_values, preferred_element_type=F32
    )
    log_total = peak_new + jnp.log(total_new)
    attn = (
        (accum_new / total_new[..., None])
        .astype(BF16)
        .transpose(2, 0, 1, 3)
        .reshape(row_count, q_heads * HD)
    )
    resid = tokens + over_heads(jnp.dot(attn, w_out, preferred_element_type=F32))
    inv_two = rms_inverse(resid)
    unit_two = resid * inv_two
    normed_two = (unit_two * mlp_gain).astype(BF16)
    gate = jnp.dot(normed_two, w_gate, preferred_element_type=F32)
    up_proj = jnp.dot(normed_two, w_up, preferred_element_type=F32)
    sigma = jax.nn.sigmoid(gate)
    silu_gate = gate * sigma
    hidden = (silu_gate * up_proj).astype(BF16)
    output = (resid + over_heads(jnp.dot(hidden, w_down, preferred_element_type=F32))).astype(BF16)
    w_query, w_key, w_value, w_out, w_gate, w_up, w_down = (
        lax.all_gather(query_weight, "dp", axis=0, tiled=True),
        lax.all_gather(key_weight, "dp", axis=0, tiled=True),
        lax.all_gather(value_weight, "dp", axis=0, tiled=True),
        lax.all_gather(output_weight, "dp", axis=1, tiled=True),
        lax.all_gather(gate_weight, "dp", axis=0, tiled=True),
        lax.all_gather(up_weight, "dp", axis=0, tiled=True),
        lax.all_gather(down_weight, "dp", axis=1, tiled=True),
    )
    d_output = cotangent[0]
    d_hidden = jnp.einsum("td,fd->tf", d_output, w_down, preferred_element_type=F32)
    grad_down = jnp.einsum("tf,td->fd", hidden, d_output, preferred_element_type=F32)
    d_gate = (d_hidden * up_proj * sigma * (1.0 + gate * (1.0 - sigma))).astype(BF16)
    d_up = (d_hidden * silu_gate).astype(BF16)
    grad_gate = jnp.einsum("td,tf->df", normed_two, d_gate, preferred_element_type=F32)
    grad_up = jnp.einsum("td,tf->df", normed_two, d_up, preferred_element_type=F32)
    partial_two = jnp.einsum("tf,df->td", d_gate, w_gate, preferred_element_type=F32) + jnp.einsum(
        "tf,df->td", d_up, w_up, preferred_element_type=F32
    )
    d_normed_two = lax.psum(partial_two, "tensor")
    grad_mlp_gain = jnp.sum(d_normed_two * unit_two, axis=0)
    d_resid = d_output.astype(F32) + norm_back(d_normed_two, unit_two, inv_two, mlp_gain)
    d_resid_b = d_resid.astype(BF16)
    grad_out = jnp.einsum("th,td->hd", attn, d_resid_b, preferred_element_type=F32)
    d_attn = jnp.einsum("td,hd->th", d_resid_b, w_out, preferred_element_type=F32).astype(BF16)
    delta = jnp.sum(
        d_attn.astype(F32).reshape(row_count, q_heads, HD)
        * attn.astype(F32).reshape(row_count, q_heads, HD),
        axis=-1,
    )
    delta_heads = delta.reshape(row_count, kv_heads, group_size).transpose(1, 2, 0)
    grouped_grad = d_attn.reshape(row_count, kv_heads, group_size, HD)
    piece_keys = lax.all_gather(key_rot, "ctx", axis=0, tiled=True)
    piece_values = lax.all_gather(value, "ctx", axis=0, tiled=True)
    piece_rows = piece_keys.shape[0]
    scores = piece_scores(piece_keys)
    probs = jnp.exp(scores - log_total[..., None])
    d_probs = jnp.einsum("qkgd,nkd->kgqn", grouped_grad, piece_values, preferred_element_type=F32)
    d_scores = (probs * (d_probs - delta_heads[..., None]) * score_scale).astype(BF16)
    d_query_acc = jnp.einsum("kgqn,nkd->kgqd", d_scores, piece_keys, preferred_element_type=F32)
    d_key_piece = jnp.einsum("kgqn,qkgd->nkd", d_scores, grouped_query, preferred_element_type=F32)
    d_value_piece = jnp.einsum(
        "kgqn,qkgd->nkd", probs.astype(BF16), grouped_grad, preferred_element_type=F32
    )
    update = jnp.stack([d_key_piece, d_value_piece])
    d_kv_home = lax.psum_scatter(update, "ctx", scatter_dimension=1, tiled=True)
    d_query_rot = d_query_acc.transpose(2, 0, 1, 3).reshape(row_count, q_heads, HD)
    d_key_rot = d_kv_home[0]
    d_value = d_kv_home[1].astype(BF16).reshape(row_count, kv_heads * HD)
    d_query_scaled = d_query_rot * cos_heads + rotate_back(d_query_rot * sin_heads)
    d_key_scaled = d_key_rot * cos_heads + rotate_back(d_key_rot * sin_heads)
    query_gain_part = jnp.sum(d_query_scaled * query_unit, axis=(0, 1))
    key_gain_part = jnp.sum(d_key_scaled * key_unit, axis=(0, 1))
    d_query = (
        norm_back(d_query_scaled, query_unit, query_inv, query_gain)
        .astype(BF16)
        .reshape(row_count, q_heads * HD)
    )
    d_key = (
        norm_back(d_key_scaled, key_unit, key_inv, key_gain)
        .astype(BF16)
        .reshape(row_count, kv_heads * HD)
    )
    grad_query = jnp.einsum("td,th->dh", normed_one, d_query, preferred_element_type=F32)
    grad_key = jnp.einsum("td,th->dh", normed_one, d_key, preferred_element_type=F32)
    grad_value = jnp.einsum("td,th->dh", normed_one, d_value, preferred_element_type=F32)
    partial_one = jnp.einsum("th,dh->td", d_query, w_query, preferred_element_type=F32)
    partial_one = partial_one + jnp.einsum("th,dh->td", d_key, w_key, preferred_element_type=F32)
    partial_one = partial_one + jnp.einsum(
        "th,dh->td", d_value, w_value, preferred_element_type=F32
    )
    d_normed_one, query_gain_heads, key_gain_heads = lax.psum(
        (partial_one, query_gain_part, key_gain_part), "tensor"
    )
    grad_attn_gain = jnp.sum(d_normed_one * unit_one, axis=0)
    d_input = (d_resid + norm_back(d_normed_one, unit_one, inv_one, attn_gain)).astype(BF16)
    (
        share_a,
        share_q,
        share_k,
        share_v,
        share_qg,
        share_kg,
        share_o,
        share_m,
        share_g,
        share_u,
        share_d,
    ) = (
        lax.psum_scatter(grad_attn_gain, "dp", scatter_dimension=0, tiled=True),
        lax.psum_scatter(grad_query, "dp", scatter_dimension=0, tiled=True),
        lax.psum_scatter(grad_key, "dp", scatter_dimension=0, tiled=True),
        lax.psum_scatter(grad_value, "dp", scatter_dimension=0, tiled=True),
        lax.psum_scatter(query_gain_heads, "dp", scatter_dimension=0, tiled=True),
        lax.psum_scatter(key_gain_heads, "dp", scatter_dimension=0, tiled=True),
        lax.psum_scatter(grad_out, "dp", scatter_dimension=1, tiled=True),
        lax.psum_scatter(grad_mlp_gain, "dp", scatter_dimension=0, tiled=True),
        lax.psum_scatter(grad_gate, "dp", scatter_dimension=0, tiled=True),
        lax.psum_scatter(grad_up, "dp", scatter_dimension=0, tiled=True),
        lax.psum_scatter(grad_down, "dp", scatter_dimension=1, tiled=True),
    )
    finals = lax.psum(
        (
            share_a,
            share_q,
            share_k,
            share_v,
            share_qg,
            share_kg,
            share_o,
            share_m,
            share_g,
            share_u,
            share_d,
        ),
        "ctx",
    )
    return (
        output[None],
        d_input[None],
        finals[0],
        finals[1],
        finals[2],
        finals[3],
        finals[4],
        finals[5],
        finals[6],
        finals[7],
        finals[8],
        finals[9],
        finals[10],
    )


def tree_exchange(value, axis_name, axis_size):
    return lax.ppermute(value, axis_name, [(i, i ^ 1) for i in range(axis_size)])


def paired_device(
    dp_size,
    block_input,
    attn_gain,
    query_weight,
    key_weight,
    value_weight,
    query_gain,
    key_gain,
    output_weight,
    mlp_gain,
    gate_weight,
    up_weight,
    down_weight,
    cotangent,
):
    line = dp_size // 2
    line_groups = [[2 * j + side for j in range(line)] for side in range(2)]
    side = lax.axis_index("dp") % 2
    block = lax.axis_index("ctx")
    owned = query_weight.shape[0]
    width = owned * dp_size

    def to_ctx(value):
        return tree_exchange(value, "ctx", 2)

    def to_pair(value):
        return tree_exchange(value, "dp", dp_size)

    def over_tensor(value):
        return value + tree_exchange(value, "tensor", 2)

    def to_local(value):
        split = value.reshape(value.shape[:-1] + (line, 2, owned))
        first, second = split[..., 0, :], split[..., 1, :]
        ordered = jnp.where(
            side == 0,
            jnp.stack([first, second], axis=-3),
            jnp.stack([second, first], axis=-3),
        )
        return ordered.reshape(value.shape)

    def from_local(value):
        split = value.reshape(value.shape[:-1] + (2, line, owned))
        first, second = split[..., 0, :, :], split[..., 1, :, :]
        ordered = jnp.where(
            side == 0,
            jnp.stack([first, second], axis=-2),
            jnp.stack([second, first], axis=-2),
        )
        return ordered.reshape(value.shape)

    def own_half(shard):
        half = shard.shape[1] // 2
        return lax.dynamic_slice_in_dim(shard, block * half, half, axis=1)

    def gather_line(shard):
        return lax.all_gather(
            shard, "dp", axis_index_groups=line_groups, axis=0, tiled=True
        )

    def to_diagonal(value):
        steps = [(i, i ^ 3) for i in range(2 * dp_size)]
        return lax.ppermute(value, ("dp", "ctx"), steps)

    def gather(shards):
        shards = [own_half(shard) for shard in shards]
        part = gather_line(jnp.concatenate(shards, axis=1))
        over_ctx, over_pair = to_ctx(part), to_pair(part)
        middle = part.shape[1] // 2
        diagonal = jnp.concatenate(
            [to_ctx(over_pair[:, :middle]), to_pair(over_ctx[:, middle:])], axis=1
        )
        found, low = [], 0
        for shard in shards:
            high = low + shard.shape[1]
            top = jnp.concatenate([part[:, low:high], over_ctx[:, low:high]], axis=1)
            bottom = jnp.concatenate([over_pair[:, low:high], diagonal[:, low:high]], axis=1)
            found.append(jnp.concatenate([top, bottom], axis=0))
            low = high
        return found

    w_query, w_key, w_value = gather([query_weight, key_weight, value_weight])
    w_out_t, w_gate = gather([output_weight.T, gate_weight])
    w_up, w_down_t = gather([up_weight, down_weight.T])

    def feature_side(value):
        half = value.shape[1] // 2
        own, far = value[:, :half], value[:, half:]
        return jnp.concatenate([own, to_ctx(own), to_pair(far), to_diagonal(far)], axis=0)

    def column_side(values):
        own = jnp.concatenate([value[:, : value.shape[1] // 2] for value in values], axis=1)
        far = jnp.concatenate([value[:, value.shape[1] // 2 :] for value in values], axis=1)
        return jnp.concatenate([own, to_ctx(far), to_pair(own), to_diagonal(far)], axis=0)

    def weight_share(features, columns):
        part = jnp.einsum("td,tf->df", features, columns, preferred_element_type=F32)
        share = lax.psum_scatter(
            part, "dp", axis_index_groups=line_groups, scatter_dimension=0, tiled=True
        )
        return share, to_ctx(share)

    def whole(share, other):
        return jnp.where(
            block == 0,
            jnp.concatenate([share, other], axis=1),
            jnp.concatenate([other, share], axis=1),
        )

    def mul_t(value, weight):
        return jnp.einsum("tf,df->td", value, weight, preferred_element_type=F32)

    row_count = block_input.shape[1]
    score_scale = 1.0 / math.sqrt(HD)
    attn_gain = to_local(attn_gain)
    mlp_gain = to_local(mlp_gain)
    tokens = to_local(block_input[0]).astype(F32)
    d_output = to_local(cotangent[0])
    positions = block * row_count + jnp.arange(row_count, dtype=jnp.int32)
    other_positions = (1 - block) * row_count + jnp.arange(row_count, dtype=jnp.int32)
    cos_table, sin_table = rope_tables(positions, HD)
    cos_heads = cos_table[:, None, :]
    sin_heads = sin_table[:, None, :]
    q_heads = w_query.shape[1] // HD
    kv_heads = w_key.shape[1] // HD
    group_size = q_heads // kv_heads

    inv_one = rms_inverse(tokens)
    unit_one = tokens * inv_one
    normed_one = (unit_one * attn_gain).astype(BF16)
    query = jnp.dot(normed_one, w_query, preferred_element_type=F32).reshape(row_count, q_heads, HD)
    key_raw = jnp.dot(normed_one, w_key, preferred_element_type=F32).reshape(
        row_count, kv_heads, HD
    )
    value = (
        jnp.dot(normed_one, w_value, preferred_element_type=F32)
        .astype(BF16)
        .reshape(row_count, kv_heads, HD)
    )
    query_inv = rms_inverse(query)
    query_unit = query * query_inv
    query_scaled = query_unit * query_gain
    query_rot = (query_scaled * cos_heads + rotate(query_scaled) * sin_heads).astype(BF16)
    key_inv = rms_inverse(key_raw)
    key_unit = key_raw * key_inv
    key_scaled = key_unit * key_gain
    key_rot = (key_scaled * cos_heads + rotate(key_scaled) * sin_heads).astype(BF16)
    grouped_query = query_rot.reshape(row_count, kv_heads, group_size, HD)

    def swap_heads(array):
        half = array.shape[-2] // 2
        return jnp.concatenate([array[..., half:, :], array[..., :half, :]], axis=-2)

    other_keys = swap_heads(to_ctx(key_rot))
    other_values = swap_heads(to_ctx(value))
    all_keys = jnp.concatenate([key_rot, other_keys], axis=0)
    all_values = jnp.concatenate([value, other_values], axis=0)
    key_positions = jnp.concatenate([positions, other_positions])
    allowed = key_positions[None, :] <= positions[:, None]
    scores = (
        jnp.einsum("qkgd,nkd->kgqn", grouped_query, all_keys, preferred_element_type=F32)
        * score_scale
    )
    scores = jnp.where(allowed, scores, -jnp.inf)
    peak = jnp.max(scores, axis=-1)
    expo = jnp.exp(scores - peak[..., None])
    total = jnp.sum(expo, axis=-1)
    accum = jnp.einsum("kgqn,nkd->kgqd", expo.astype(BF16), all_values, preferred_element_type=F32)
    log_total = peak + jnp.log(total)
    attn = (
        (accum / total[..., None])
        .astype(BF16)
        .transpose(2, 0, 1, 3)
        .reshape(row_count, q_heads * HD)
    )
    resid = tokens + over_tensor(mul_t(attn, w_out_t))
    inv_two = rms_inverse(resid)
    unit_two = resid * inv_two
    normed_two = (unit_two * mlp_gain).astype(BF16)
    features_down = feature_side(d_output)
    features_two = feature_side(normed_two)
    columns_out = column_side([attn])
    gate = jnp.dot(normed_two, w_gate, preferred_element_type=F32)
    up_proj = jnp.dot(normed_two, w_up, preferred_element_type=F32)
    sigma = jax.nn.sigmoid(gate)
    silu_gate = gate * sigma
    hidden = (silu_gate * up_proj).astype(BF16)
    output = from_local((resid + over_tensor(mul_t(hidden, w_down_t))).astype(BF16))

    features_down, hidden = lax.optimization_barrier((features_down, hidden))
    share_down = weight_share(features_down, column_side([hidden]))
    d_hidden = jnp.dot(d_output, w_down_t, preferred_element_type=F32)
    d_gate = (d_hidden * up_proj * sigma * (1.0 + gate * (1.0 - sigma))).astype(BF16)
    d_up = (d_hidden * silu_gate).astype(BF16)
    features_two, columns_out, d_gate, d_up = lax.optimization_barrier(
        (features_two, columns_out, d_gate, d_up)
    )
    share_mlp, other_mlp = weight_share(features_two, column_side([d_gate, d_up]))
    d_normed_two = over_tensor(mul_t(d_gate, w_gate) + mul_t(d_up, w_up))
    grad_mlp_gain = jnp.sum(d_normed_two * unit_two, axis=0)
    d_resid = d_output.astype(F32) + norm_back(d_normed_two, unit_two, inv_two, mlp_gain)
    d_resid_b = d_resid.astype(BF16)
    share_out = weight_share(feature_side(d_resid_b), columns_out)
    d_attn = jnp.dot(d_resid_b, w_out_t, preferred_element_type=F32).astype(BF16)
    delta = jnp.sum(
        d_attn.astype(F32).reshape(row_count, q_heads, HD)
        * attn.astype(F32).reshape(row_count, q_heads, HD),
        axis=-1,
    )
    delta_heads = delta.reshape(row_count, kv_heads, group_size).transpose(1, 2, 0)
    grouped_grad = d_attn.reshape(row_count, kv_heads, group_size, HD)
    probs = jnp.exp(scores - log_total[..., None])
    d_probs = jnp.einsum("qkgd,nkd->kgqn", grouped_grad, all_values, preferred_element_type=F32)
    d_scores = (probs * (d_probs - delta_heads[..., None]) * score_scale).astype(BF16)
    d_query_acc = jnp.einsum("kgqn,nkd->kgqd", d_scores, all_keys, preferred_element_type=F32)
    d_keys = jnp.einsum("kgqn,qkgd->nkd", d_scores, grouped_query, preferred_element_type=F32)
    d_values = jnp.einsum(
        "kgqn,qkgd->nkd", probs.astype(BF16), grouped_grad, preferred_element_type=F32
    )
    d_key_rot = d_keys[:row_count] + swap_heads(to_ctx(d_keys[row_count:]))
    d_value_sum = d_values[:row_count] + swap_heads(to_ctx(d_values[row_count:]))
    d_query_rot = d_query_acc.transpose(2, 0, 1, 3).reshape(row_count, q_heads, HD)
    d_value = d_value_sum.astype(BF16).reshape(row_count, kv_heads * HD)
    d_query_scaled = d_query_rot * cos_heads + rotate_back(d_query_rot * sin_heads)
    d_key_scaled = d_key_rot * cos_heads + rotate_back(d_key_rot * sin_heads)
    query_gain_part = jnp.sum(d_query_scaled * query_unit, axis=(0, 1))
    key_gain_part = jnp.sum(d_key_scaled * key_unit, axis=(0, 1))
    d_query = (
        norm_back(d_query_scaled, query_unit, query_inv, query_gain)
        .astype(BF16)
        .reshape(row_count, q_heads * HD)
    )
    d_key = (
        norm_back(d_key_scaled, key_unit, key_inv, key_gain)
        .astype(BF16)
        .reshape(row_count, kv_heads * HD)
    )
    features_one = feature_side(normed_one)
    features_one, share_down, d_query, d_key, d_value = lax.optimization_barrier(
        (features_one, share_down, d_query, d_key, d_value)
    )
    columns_one = column_side([d_query, d_key, d_value])
    share_qkv, other_qkv_share = weight_share(features_one, columns_one)
    d_normed_one = over_tensor(
        mul_t(d_query, w_query) + mul_t(d_key, w_key) + mul_t(d_value, w_value)
    )
    grad_attn_gain = jnp.sum(d_normed_one * unit_one, axis=0)
    d_input = from_local(
        (d_resid + norm_back(d_normed_one, unit_one, inv_one, attn_gain)).astype(BF16)
    )
    gains = over_tensor(
        jnp.concatenate(
            [
                from_local(0.5 * grad_attn_gain),
                from_local(0.5 * grad_mlp_gain),
                query_gain_part,
                key_gain_part,
            ]
        )
    )
    share_mlp, other_mlp, share_out, gains = lax.optimization_barrier(
        (share_mlp, other_mlp, share_out, gains)
    )
    gains = gains + to_ctx(gains)
    stride = 1
    while stride < dp_size:
        gains = gains + lax.ppermute(gains, "dp", [(i, i ^ stride) for i in range(dp_size)])
        stride *= 2
    owner = lax.axis_index("dp")

    def owned_gain(start, size):
        part = size // dp_size
        return lax.dynamic_slice_in_dim(gains, start + owner * part, part)

    def qkv_piece(low, high):
        return whole(share_qkv[:, low:high], other_qkv_share[:, low:high])

    cut_q = query_weight.shape[1] // 2
    cut_k = cut_q + key_weight.shape[1] // 2
    cut_g = gate_weight.shape[1] // 2

    return (
        output[None],
        d_input[None],
        owned_gain(0, width),
        qkv_piece(0, cut_q),
        qkv_piece(cut_q, cut_k),
        qkv_piece(cut_k, share_qkv.shape[1]),
        owned_gain(2 * width, HD),
        owned_gain(2 * width + HD, HD),
        whole(*share_out).T,
        owned_gain(width, width),
        whole(share_mlp[:, :cut_g], other_mlp[:, :cut_g]),
        whole(share_mlp[:, cut_g:], other_mlp[:, cut_g:]),
        whole(*share_down).T,
    )


def solution(mesh):
    sizes = dict(mesh.shape)
    body = per_device
    if sizes["ctx"] == 2 and sizes["tensor"] == 2 and sizes["dp"] in (2, 4, 8, 16):
        body = functools.partial(paired_device, sizes["dp"])
    return jax.shard_map(
        body,
        mesh=mesh,
        in_specs=(
            P("dp", "ctx", None),
            P(),
            P("dp", "tensor"),
            P("dp", "tensor"),
            P("dp", "tensor"),
            P(),
            P(),
            P("tensor", "dp"),
            P(),
            P("dp", "tensor"),
            P("dp", "tensor"),
            P("tensor", "dp"),
            P("dp", "ctx", None),
        ),
        out_specs=(
            P("dp", "ctx", None),
            P("dp", "ctx", None),
            P("dp"),
            P("dp", "tensor"),
            P("dp", "tensor"),
            P("dp", "tensor"),
            P("dp"),
            P("dp"),
            P("tensor", "dp"),
            P("dp"),
            P("dp", "tensor"),
            P("dp", "tensor"),
            P("tensor", "dp"),
        ),
        check_vma=False,
    )
```
